32 devices in a mesh: rep: 2 (over core), shard: 4 (over y, x), ctx: 4 (over z).
Axes of the slice: x: 2, y: 2, z: 4, core: 2. Of those that a mesh axis runs over, the one named last changes fastest.
Arguments:
- inputs: bfloat16 [8, 1152, 1536], P(('rep', 'shard'), 'ctx'), may hold values from -6 to 6
- segment_ids: int32 [8, 1152], P(('rep', 'shard'), 'ctx'), may hold values from 0 to 19, as said below
- cotangent: bfloat16 [8, 1152, 1536], P(('rep', 'shard'), 'ctx'), may hold values from -6 to 6
- attn_gain_one: bfloat16 [1536], P(('shard', 'ctx')), may hold values from 0.5 to 1.5
- query_one: bfloat16 [1536, 1536], P(('shard', 'ctx')), may hold values from -0.15625 to 0.15625
- first_key_matrix: bfloat16 [1536, 768], P(('shard', 'ctx')), may hold values from -0.15625 to 0.15625
- first_value_matrix: bfloat16 [1536, 768], P(('shard', 'ctx')), may hold values from -0.15625 to 0.15625
- out_one: bfloat16 [1536, 1536], P(('shard', 'ctx')), may hold values from -1.25 to 1.25
- mlp_gain_one: bfloat16 [1536], P(('shard', 'ctx')), may hold values from 0.5 to 1.5
- gate_one: bfloat16 [1536, 4096], P(('shard', 'ctx')), may hold values from -0.15625 to 0.15625
- up_one: bfloat16 [1536, 4096], P(('shard', 'ctx')), may hold values from -0.15625 to 0.15625
- down_one: bfloat16 [4096, 1536], P(('shard', 'ctx')), may hold values from -0.09375 to 0.09375
- attn_gain_two: bfloat16 [1536], P(('shard', 'ctx')), may hold values from 0.5 to 1.5
- query_two: bfloat16 [1536, 1536], P(('shard', 'ctx')), may hold values from -0.15625 to 0.15625
- second_key_matrix: bfloat16 [1536, 768], P(('shard', 'ctx')), may hold values from -0.15625 to 0.15625
- second_value_matrix: bfloat16 [1536, 768], P(('shard', 'ctx')), may hold values from -0.15625 to 0.15625
- out_two: bfloat16 [1536, 1536], P(('shard', 'ctx')), may hold values from -1.25 to 1.25
- mlp_gain_two: bfloat16 [1536], P(('shard', 'ctx')), may hold values from 0.5 to 1.5
- gate_two: bfloat16 [1536, 4096], P(('shard', 'ctx')), may hold values from -0.15625 to 0.15625
- up_two: bfloat16 [1536, 4096], P(('shard', 'ctx')), may hold values from -0.15625 to 0.15625
- down_two: bfloat16 [4096, 1536], P(('shard', 'ctx')), may hold values from -0.09375 to 0.09375
Outputs:
- activations: float32 [8, 1152, 1536], P(('rep', 'shard'), 'ctx')
- input_grad: float32 [8, 1152, 1536], P(('rep', 'shard'), 'ctx')
- grad_attn_gain_one: float32 [1536], P(('shard', 'ctx'))
- grad_query_one: float32 [1536, 1536], P(('shard', 'ctx'))
- grad_key_one: float32 [1536, 768], P(('shard', 'ctx'))
- grad_value_one: float32 [1536, 768], P(('shard', 'ctx'))
- grad_out_one: float32 [1536, 1536], P(('shard', 'ctx'))
- grad_mlp_gain_one: float32 [1536], P(('shard', 'ctx'))
- grad_gate_one: float32 [1536, 4096], P(('shard', 'ctx'))
- grad_up_one: float32 [1536, 4096], P(('shard', 'ctx'))
- grad_down_one: float32 [4096, 1536], P(('shard', 'ctx'))
- grad_attn_gain_two: float32 [1536], P(('shard', 'ctx'))
- grad_query_two: float32 [1536, 1536], P(('shard', 'ctx'))
- grad_key_two: float32 [1536, 768], P(('shard', 'ctx'))
- grad_value_two: float32 [1536, 768], P(('shard', 'ctx'))
- grad_out_two: float32 [1536, 1536], P(('shard', 'ctx'))
- grad_mlp_gain_two: float32 [1536], P(('shard', 'ctx'))
- grad_gate_two: float32 [1536, 4096], P(('shard', 'ctx'))
- grad_up_two: float32 [1536, 4096], P(('shard', 'ctx'))
- grad_down_two: float32 [4096, 1536], P(('shard', 'ctx'))
The draws below stay inside these ranges and needn't reach their ends.
Inputs may be any that keep to these rules, and one draw needn't show every extreme that they name: `segment_ids`: each sequence holds whole documents numbered 1, 2, 3, ... in order from its first token, followed by padding numbered 0 where the last document does not reach its end; documents are 60 tokens or more (2 at the least), and the first sequence is packed with documents of that shortest length.
All inputs are finite; a program needn't handle non-finite values.
Results may differ from the reference program's by a relative error of at most 0.025.
Values may be sent and summed in bfloat16 or wider, within the bound.
No kernel may reach another device: no remote copies, remote signals or barrier semaphores. Data moves between devices by JAX's collectives and lax.ppermute only.
A program may use at most 448 MiB of HBM per device.

```python
import math
import jax
import jax.numpy as jnp
from jax import lax

MODEL_DIM = 1536
QUERY_HEADS = 16
KEY_VALUE_HEADS = 8
HEAD_DIM = 96
FF = 4096
LEN = 1152
SEQS = 8


def draw_segment_ids(key, part):
    shortest = max(2, LEN * 60 // 1152)
    longest = max(shortest + 1, LEN * 800 // 1152)
    doc_count = LEN // shortest + 1
    doc_sizes = jax.random.randint(key, (SEQS, doc_count), shortest, longest + 1, dtype=jnp.int32)
    seq_index = jnp.arange(SEQS, dtype=jnp.int32)
    doc_sizes = jnp.where(seq_index[:, None] == 0, jnp.int32(shortest), doc_sizes).astype(jnp.int32)
    doc_ends = jnp.cumsum(doc_sizes, axis=1).astype(jnp.int32)
    position = jnp.arange(LEN, dtype=jnp.int32)
    doc_index = jnp.sum((doc_ends[:, None, :] <= position[None, :, None]).astype(jnp.int32), axis=2)
    end_of_doc = jnp.take_along_axis(doc_ends, doc_index, axis=1)
    return jnp.where(end_of_doc <= LEN, doc_index + 1, 0).astype(jnp.int32)


def levels(rng, extent, shards, smallest, largest):
    loudness, own = 1.0, jax.random.fold_in(rng, 6)
    for dim, shards_of in shards:
        draws = jnp.exp(jax.random.uniform(jax.random.fold_in(own, dim), (shards_of,), jnp.float32, smallest / len(shards), largest / len(shards)))
        loudness = loudness * jnp.repeat(draws, extent[dim] // shards_of).reshape([-1 if axis == dim else 1 for axis in range(len(extent))])
    return loudness


def scatter_about(own_key, shape, deviation, reach, pieces=(), held_as=jnp.bfloat16):
    drawn = jax.random.normal(own_key, shape, jnp.float32) * deviation
    if len(pieces) > 0:
        drawn = levels(own_key, shape, pieces, -0.22, 0.18) * drawn
    return jnp.clip(drawn, min=-reach, max=reach).astype(held_as)


def setup_inputs(seed: int = 0) -> dict:
    keys = jax.random.split(jax.random.key(seed), 22)
    return {
        "inputs": scatter_about(keys[0], (SEQS, LEN, MODEL_DIM), 1.0, 6.0, ((0, 8), (1, 4))),
        "segment_ids": draw_segment_ids(jax.random.fold_in(keys[21], 71), 0),
        "cotangent": scatter_about(keys[2], (SEQS, LEN, MODEL_DIM), 1.0, 6.0, ((0, 8), (1, 4))),
        "attn_gain_one": jnp.clip(1.0 + 0.1 * jax.random.normal(keys[3], (MODEL_DIM,), jnp.float32), 0.5, 1.5).astype(jnp.bfloat16),
        "query_one": scatter_about(keys[4], (MODEL_DIM, QUERY_HEADS * HEAD_DIM), MODEL_DIM ** -0.5, 0.15625, ((0, 16),)),
        "first_key_matrix": scatter_about(keys[5], (MODEL_DIM, KEY_VALUE_HEADS * HEAD_DIM), MODEL_DIM ** -0.5, 0.15625, ((0, 16),)),
        "first_value_matrix": scatter_about(keys[6], (MODEL_DIM, KEY_VALUE_HEADS * HEAD_DIM), MODEL_DIM ** -0.5, 0.15625, ((0, 16),)),
        "out_one": scatter_about(keys[7], (QUERY_HEADS * HEAD_DIM, MODEL_DIM), (max(1, QUERY_HEADS * HEAD_DIM // 64)) ** -0.5, 1.25, ((0, 16),)),
        "mlp_gain_one": jnp.clip(1.0 + 0.1 * jax.random.normal(keys[8], (MODEL_DIM,), jnp.float32), 0.5, 1.5).astype(jnp.bfloat16),
        "gate_one": scatter_about(keys[9], (MODEL_DIM, FF), MODEL_DIM ** -0.5, 0.15625, ((0, 16),)),
        "up_one": scatter_about(keys[10], (MODEL_DIM, FF), MODEL_DIM ** -0.5, 0.15625, ((0, 16),)),
        "down_one": scatter_about(keys[11], (FF, MODEL_DIM), FF ** -0.5, 0.09375, ((0, 16),)),
        "attn_gain_two": jnp.clip(1.0 + 0.1 * jax.random.normal(keys[12], (MODEL_DIM,), jnp.float32), 0.5, 1.5).astype(jnp.bfloat16),
        "query_two": scatter_about(keys[13], (MODEL_DIM, QUERY_HEADS * HEAD_DIM), MODEL_DIM ** -0.5, 0.15625, ((0, 16),)),
        "second_key_matrix": scatter_about(keys[14], (MODEL_DIM, KEY_VALUE_HEADS * HEAD_DIM), MODEL_DIM ** -0.5, 0.15625, ((0, 16),)),
        "second_value_matrix": scatter_about(keys[15], (MODEL_DIM, KEY_VALUE_HEADS * HEAD_DIM), MODEL_DIM ** -0.5, 0.15625, ((0, 16),)),
        "out_two": scatter_about(keys[16], (QUERY_HEADS * HEAD_DIM, MODEL_DIM), (max(1, QUERY_HEADS * HEAD_DIM // 64)) ** -0.5, 1.25, ((0, 16),)),
        "mlp_gain_two": jnp.clip(1.0 + 0.1 * jax.random.normal(keys[17], (MODEL_DIM,), jnp.float32), 0.5, 1.5).astype(jnp.bfloat16),
        "gate_two": scatter_about(keys[18], (MODEL_DIM, FF), MODEL_DIM ** -0.5, 0.15625, ((0, 16),)),
        "up_two": scatter_about(keys[19], (MODEL_DIM, FF), MODEL_DIM ** -0.5, 0.15625, ((0, 16),)),
        "down_two": scatter_about(keys[20], (FF, MODEL_DIM), FF ** -0.5, 0.09375, ((0, 16),)),
    }


epsilon = 1e-05
rope_base = 100000.0

@jax.custom_vjp
def lowered_forward(v):
    return lax.optimization_barrier(v.astype(jnp.bfloat16)).astype(jnp.float32)

@jax.custom_vjp
def lowered_backward(v):
    return v

def low_keep(v):
    return (lowered_forward(v), None)

def low_pass(kept, grad):
    return (grad,)

def back_keep(v):
    return (v, None)

def back_low(kept, grad):
    return (lowered_forward(grad),)
lowered_forward.defvjp(low_keep, low_pass)
lowered_backward.defvjp(back_keep, back_low)

def matrix_product(left_mat, right_mat):
    return jnp.dot(left_mat, right_mat, precision=lax.Precision.HIGHEST)

def rotate(values, cosine, sine_table):
    half_dim = values.shape[-1] // 2
    turned = jnp.concatenate([-values[..., half_dim:], values[..., :half_dim]], axis=-1)
    return values * cosine + turned * sine_table

def rms_norm(hidden, norm_gain):
    inv_rms = lax.rsqrt(lax.optimization_barrier(jnp.mean(hidden * hidden, axis=-1, keepdims=True)) + epsilon)
    return lowered_forward(hidden * inv_rms * norm_gain)

def make_tables(segments):
    sequence_length = segments.shape[1]
    token_index = jnp.arange(sequence_length, dtype=jnp.int32)
    same_doc = segments[:, :, None] == segments[:, None, :]
    doc_start = lax.optimization_barrier(jnp.min(jnp.where(same_doc, token_index[None, None, :], sequence_length), axis=2))
    position = (token_index[None, :] - doc_start).astype(jnp.float32)
    inv_freq = rope_base ** (-jnp.arange(0, HEAD_DIM, 2, dtype=jnp.float32) / HEAD_DIM)
    angles = position[:, :, None] * inv_freq
    cosine = jnp.concatenate([jnp.cos(angles), jnp.cos(angles)], axis=-1)
    sine_table = jnp.concatenate([jnp.sin(angles), jnp.sin(angles)], axis=-1)
    allowed = same_doc & (token_index[None, None, :] <= token_index[None, :, None])
    return (cosine, sine_table, allowed)

def one_layer(hidden, weights, cosine, sine_table, allowed):
    attn_gain, query_weight_matrix, key_weight_matrix, value_weight_matrix, w_out, mlp_gain, w_gate, w_up, w_down = weights
    sequence_total, sequence_length, model_width = hidden.shape
    heads_per_group = QUERY_HEADS // KEY_VALUE_HEADS
    attention_input = rms_norm(hidden, attn_gain)
    query_projected = lowered_backward(matrix_product(attention_input, query_weight_matrix)).reshape(sequence_total, sequence_length, KEY_VALUE_HEADS, heads_per_group, HEAD_DIM)
    key_projected = lowered_backward(matrix_product(attention_input, key_weight_matrix)).reshape(sequence_total, sequence_length, KEY_VALUE_HEADS, HEAD_DIM)
    value_projected = lowered_forward(lowered_backward(matrix_product(attention_input, value_weight_matrix))).reshape(sequence_total, sequence_length, KEY_VALUE_HEADS, HEAD_DIM)
    query_rot = lowered_forward(rotate(query_projected, cosine[:, :, None, None, :], sine_table[:, :, None, None, :]))
    key_rot = lowered_forward(rotate(key_projected, cosine[:, :, None, :], sine_table[:, :, None, :]))
    raw_scores = jnp.einsum('bqkgd,btkd->bkgqt', query_rot, key_rot, precision=lax.Precision.HIGHEST)
    scores = lowered_backward(raw_scores * (1.0 / math.sqrt(HEAD_DIM)))
    scores = jnp.where(allowed[:, None, None], scores, -1e+30)
    probs = lowered_forward(jax.nn.softmax(scores, axis=-1))
    attended = jnp.einsum('bkgqt,btkd->bqkgd', probs, value_projected, precision=lax.Precision.HIGHEST)
    attended = lowered_forward(lowered_backward(attended)).reshape(sequence_total, sequence_length, QUERY_HEADS * HEAD_DIM)
    middle = hidden + lowered_backward(matrix_product(attended, w_out))
    mlp_in = rms_norm(middle, mlp_gain)
    gate_proj = lowered_backward(matrix_product(mlp_in, w_gate))
    up_proj = lowered_backward(matrix_product(mlp_in, w_up))
    mixed_act = lowered_forward(jax.nn.silu(gate_proj) * up_proj)
    return middle + lowered_backward(matrix_product(mixed_act, w_down))

def reference(inputs, segment_ids, cotangent, attn_gain_one, query_one, first_key_matrix, first_value_matrix, out_one, mlp_gain_one, gate_one, up_one, down_one, attn_gain_two, query_two, second_key_matrix, second_value_matrix, out_two, mlp_gain_two, gate_two, up_two, down_two):
    weights = jax.tree.map(lambda weight_arr: weight_arr.astype(jnp.float32), (attn_gain_one, query_one, first_key_matrix, first_value_matrix, out_one, mlp_gain_one, gate_one, up_one, down_one, attn_gain_two, query_two, second_key_matrix, second_value_matrix, out_two, mlp_gain_two, gate_two, up_two, down_two))
    input_groups = inputs.astype(jnp.float32).reshape(SEQS, 1, LEN, MODEL_DIM)
    id_groups = segment_ids.reshape(SEQS, 1, LEN)
    cot_groups = cotangent.astype(jnp.float32).reshape(SEQS, 1, LEN, MODEL_DIM)

    def one_step(grad_sums, batch_item):
        input_pair, ids_pair, cot_pair = batch_item
        cosine, sine_table, allowed = make_tables(ids_pair)

        def forward(x_input, all_weights):
            hidden = one_layer(x_input, all_weights[:9], cosine, sine_table, allowed)
            return one_layer(hidden, all_weights[9:], cosine, sine_table, allowed)
        output, pullback = jax.vjp(forward, input_pair, weights)
        grad_input, grad_weights = pullback(cot_pair)
        return (jax.tree.map(jnp.add, grad_sums, grad_weights), (output, grad_input))
    zero_sums = jax.tree.map(jnp.zeros_like, weights)
    grad_sums, (outputs, grad_inputs) = lax.scan(one_step, zero_sums, (input_groups, id_groups, cot_groups))
    return (outputs.reshape(SEQS, LEN, MODEL_DIM), grad_inputs.reshape(SEQS, LEN, MODEL_DIM), grad_sums[0], grad_sums[1], grad_sums[2], grad_sums[3], grad_sums[4], grad_sums[5], grad_sums[6], grad_sums[7], grad_sums[8], grad_sums[9], grad_sums[10], grad_sums[11], grad_sums[12], grad_sums[13], grad_sums[14], grad_sums[15], grad_sums[16], grad_sums[17])
```

```python
import math

import jax
import jax.numpy as jnp
from jax import lax
from jax.sharding import PartitionSpec as P

HEAD_DIM = 96

epsilon = 1e-05
rope_base = 100000.0

BF = jnp.bfloat16
F32 = jnp.float32
GROUP = ("shard", "ctx")


def mul(left, right):
    return jnp.dot(left, right, preferred_element_type=F32)


def contract(left_mat, right_mat):
    return lax.dot_general(
        left_mat, right_mat, (((0,), (0,)), ((), ())), preferred_element_type=F32
    )


def by_transpose(left_mat, right_mat):
    return lax.dot_general(
        left_mat, right_mat, (((1,), (1,)), ((), ())), preferred_element_type=F32
    )


def swap(value):
    return lax.ppermute(value, "rep", [(0, 1), (1, 0)])


def gather(block):
    return lax.all_gather(block, GROUP, axis=0, tiled=True)


def scatter(total):
    return lax.psum_scatter(total, GROUP, scatter_dimension=0, tiled=True)


def arrange(first, mine, other):
    return jnp.where(first, mine, other), jnp.where(first, other, mine)


def natural(first, mine, other):
    return jnp.concatenate(arrange(first, mine, other), axis=-1)


def divide(first, value):
    half = value.shape[-1] // 2
    return arrange(first, value[:, :half], value[:, half:])


def rms_parts(hidden, norm_gain):
    inv_rms = lax.rsqrt(jnp.mean(hidden * hidden, axis=-1, keepdims=True) + epsilon)
    return inv_rms, (hidden * inv_rms * norm_gain).astype(BF)


def rms_back(grad_in, hidden, inv_rms, norm_gain):
    normed = hidden * inv_rms
    gain_grad = jnp.sum(grad_in * normed, axis=0)
    grad_normed = grad_in * norm_gain
    back_flow = inv_rms * (
        grad_normed - normed * jnp.mean(grad_normed * normed, axis=-1, keepdims=True)
    )
    return (back_flow, gain_grad)


def rotate(values, cosine, sine_table):
    half_dim = values.shape[-1] // 2
    turned = jnp.concatenate([-values[..., half_dim:], values[..., :half_dim]], axis=-1)
    return values * cosine + turned * sine_table


def unrotate(grads, cosine, sine_table):
    half_dim = grads.shape[-1] // 2
    scaled_sin = grads * sine_table
    turned = jnp.concatenate([scaled_sin[..., half_dim:], -scaled_sin[..., :half_dim]], axis=-1)
    return grads * cosine + turned


def scaled_scores(query_rot, key_all, allowed):
    raw_scores = jnp.einsum("qkgd,tkd->kgqt", query_rot, key_all, preferred_element_type=F32)
    return jnp.where(allowed[None, None], raw_scores * (1.0 / math.sqrt(HEAD_DIM)), -1e30)


def layer_forward(hidden, gains, weights, tables, first):
    attn_gain, mlp_gain = gains
    qkv, out_w, gate_w, up_w, down_w = weights
    cosine, sine, allowed = tables
    length = hidden.shape[0]
    wide = qkv[0].shape[1]
    q_cols, kv_cols = wide // 2, wide // 4
    inv_a, attn_in = rms_parts(hidden, attn_gain)
    made = [mul(attn_in, w) for w in qkv]
    query = jnp.concatenate([m[:, :q_cols] for m in made], axis=1)
    key = jnp.concatenate([m[:, q_cols : q_cols + kv_cols] for m in made], axis=1)
    value = jnp.concatenate([m[:, q_cols + kv_cols :] for m in made], axis=1)
    heads_kv = 2 * kv_cols // HEAD_DIM
    group = q_cols // kv_cols
    query_rot = rotate(
        query.reshape(length, heads_kv, group, HEAD_DIM),
        cosine[:, None, None],
        sine[:, None, None],
    ).astype(BF)
    key_rot = rotate(
        key.reshape(length, heads_kv, HEAD_DIM), cosine[:, None], sine[:, None]
    ).astype(BF)
    both = jnp.concatenate([key_rot.reshape(length, 2 * kv_cols), value.astype(BF)], axis=1)
    both = lax.all_gather(both, "ctx", axis=0, tiled=True)
    whole = both.shape[0]
    key_all = both[:, : 2 * kv_cols].reshape(whole, heads_kv, HEAD_DIM)
    value_all = both[:, 2 * kv_cols :].reshape(whole, heads_kv, HEAD_DIM)
    scores = scaled_scores(query_rot, key_all, allowed)
    row_max = jnp.max(scores, axis=-1, keepdims=True)
    exponent = jnp.exp(scores - row_max)
    row_sum = jnp.sum(exponent, axis=-1, keepdims=True)
    probs_low = (exponent / row_sum).astype(BF)
    log_total = row_max + jnp.log(row_sum)
    attended = jnp.einsum("kgqt,tkd->qkgd", probs_low, value_all, preferred_element_type=F32)
    attended = attended.reshape(length, 2 * q_cols).astype(BF)
    attn_out = natural(first, attended[:, :q_cols], attended[:, q_cols:])
    middle = hidden + natural(first, mul(attn_out, out_w[0]), mul(attn_out, out_w[1]))
    inv_m, mlp_in = rms_parts(middle, mlp_gain)
    output = middle
    halves = []
    for g, u, d in zip(gate_w, up_w, down_w):
        gate = mul(mlp_in, g)
        up = mul(mlp_in, u)
        mixed = (jax.nn.silu(gate) * up).astype(BF)
        output = output + mul(mixed, d)
        halves.append((gate, up, mixed))
    saved = (
        hidden,
        inv_a,
        attn_in,
        query_rot,
        key_all,
        value_all,
        log_total,
        attn_out,
        middle,
        inv_m,
        mlp_in,
        halves,
    )
    return output, saved


def reduced(parts):
    other = swap(parts(1).astype(BF))
    return scatter((parts(0) + other.astype(F32)).astype(BF))


def layer_backward(flow, gains, weights, saved, tables, first):
    attn_gain, mlp_gain = gains
    qkv, out_w, gate_w, up_w, down_w = weights
    cosine, sine, allowed = tables
    (
        hidden,
        inv_a,
        attn_in,
        query_rot,
        key_all,
        value_all,
        log_total,
        attn_out,
        middle,
        inv_m,
        mlp_in,
        halves,
    ) = saved
    length, width = flow.shape
    whole, heads_kv = key_all.shape[:2]
    wide = qkv[0].shape[1]
    q_cols, kv_cols = wide // 2, wide // 4
    group = q_cols // kv_cols
    flow_low = flow.astype(BF)
    down_grad = reduced(lambda h: contract(halves[h][2], flow_low))
    grad_gates, grad_ups = [], []
    grad_mlp_in = 0.0
    for (gate, up, mixed), g, u, d in zip(halves, gate_w, up_w, down_w):
        grad_mixed = by_transpose(flow_low, d)
        sig = jax.nn.sigmoid(gate)
        grad_gate = (grad_mixed * up * sig * (1.0 + gate * (1.0 - sig))).astype(BF)
        grad_up = (grad_mixed * (gate * sig)).astype(BF)
        grad_mlp_in = grad_mlp_in + by_transpose(grad_gate, g) + by_transpose(grad_up, u)
        grad_gates.append(grad_gate)
        grad_ups.append(grad_up)
    gate_grad = reduced(lambda h: contract(mlp_in, grad_gates[h]))
    up_grad = reduced(lambda h: contract(mlp_in, grad_ups[h]))
    back_m, mlp_gain_grad = rms_back(grad_mlp_in, middle, inv_m, mlp_gain)
    grad_middle = flow + back_m
    pieces = divide(first, grad_middle.astype(BF))
    grad_attended = by_transpose(pieces[0], out_w[0]) + by_transpose(pieces[1], out_w[1])
    mine, other = divide(first, grad_attended.astype(BF))
    grad_attended = jnp.concatenate([mine, other], axis=1).reshape(
        length, heads_kv, group, HEAD_DIM
    )
    scores = scaled_scores(query_rot, key_all, allowed)
    probs = jnp.exp(scores - log_total)
    grad_probs = jnp.einsum(
        "qkgd,tkd->kgqt", grad_attended, value_all, preferred_element_type=F32
    )
    inner_sum = jnp.sum(probs * grad_probs, axis=-1, keepdims=True)
    grad_scores = (probs * (grad_probs - inner_sum)).astype(BF)
    value_part = jnp.einsum(
        "kgqt,qkgd->tkd", probs.astype(BF), grad_attended, preferred_element_type=F32
    )
    scale = 1.0 / math.sqrt(HEAD_DIM)
    key_part = (
        jnp.einsum("kgqt,qkgd->tkd", grad_scores, query_rot, preferred_element_type=F32) * scale
    )
    both = jnp.concatenate(
        [key_part.reshape(whole, -1).astype(BF), value_part.reshape(whole, -1).astype(BF)], axis=1
    )
    both = lax.psum_scatter(both, "ctx", scatter_dimension=0, tiled=True)
    query_grad_rot = (
        jnp.einsum("kgqt,tkd->qkgd", grad_scores, key_all, preferred_element_type=F32) * scale
    )
    grad_query = (
        unrotate(query_grad_rot, cosine[:, None, None], sine[:, None, None])
        .astype(BF)
        .reshape(length, 2 * q_cols)
    )
    grad_key = (
        unrotate(
            both[:, : 2 * kv_cols].astype(F32).reshape(length, heads_kv, HEAD_DIM),
            cosine[:, None],
            sine[:, None],
        )
        .astype(BF)
        .reshape(length, 2 * kv_cols)
    )
    grad_value = both[:, 2 * kv_cols :]
    grad_made = [
        jnp.concatenate(
            [
                grad_query[:, h * q_cols : (h + 1) * q_cols],
                grad_key[:, h * kv_cols : (h + 1) * kv_cols],
                grad_value[:, h * kv_cols : (h + 1) * kv_cols],
            ],
            axis=1,
        )
        for h in (0, 1)
    ]
    grad_attn_in = by_transpose(grad_made[0], qkv[0]) + by_transpose(grad_made[1], qkv[1])
    attn_grad = reduced(
        lambda h: jnp.concatenate(
            [contract(attn_in, grad_made[h]), contract(attn_out, pieces[h])], axis=1
        )
    )
    back_a, attn_gain_grad = rms_back(grad_attn_in, hidden, inv_a, attn_gain)
    return grad_middle + back_a, (attn_gain_grad, mlp_gain_grad), (
        attn_grad,
        gate_grad,
        up_grad,
        down_grad,
    )


def body(inputs, segment_ids, cotangent, *params):
    groups, local_len, width = inputs.shape
    assert groups == 1
    rep = lax.axis_index("rep")
    first = rep == 0
    shards = lax.axis_size("shard") * lax.axis_size("ctx")
    position_of = lax.axis_index("shard") * lax.axis_size("ctx") + lax.axis_index("ctx")
    all_ids = lax.all_gather(segment_ids[0], "ctx", axis=0, tiled=True)
    own_ids = segment_ids[0]
    whole_len = all_ids.shape[0]
    query_index = lax.axis_index("ctx") * local_len + jnp.arange(local_len, dtype=jnp.int32)
    key_index = jnp.arange(whole_len, dtype=jnp.int32)
    same_doc = own_ids[:, None] == all_ids[None, :]
    doc_start = jnp.min(jnp.where(same_doc, key_index[None, :], whole_len), axis=1)
    position = (query_index - doc_start).astype(F32)
    inv_freq = rope_base ** (-jnp.arange(0, HEAD_DIM, 2, dtype=F32) / HEAD_DIM)
    angles = position[:, None] * inv_freq
    cosine = jnp.concatenate([jnp.cos(angles), jnp.cos(angles)], axis=-1)
    sine = jnp.concatenate([jnp.sin(angles), jnp.sin(angles)], axis=-1)
    allowed = same_doc & (key_index[None, :] <= query_index[:, None])
    tables = (cosine, sine, allowed)

    layers = (params[:9], params[9:])
    gain_block = jnp.concatenate([layer[i] for layer in layers for i in (0, 5)])
    all_gains = lax.all_gather(gain_block, GROUP, axis=0, tiled=True)
    all_gains = all_gains.reshape(shards, 4, -1).transpose(1, 0, 2).reshape(4, width).astype(F32)

    def columns(w):
        return lax.dynamic_slice_in_dim(w, rep * (w.shape[1] // 2), w.shape[1] // 2, 1)

    def hidden_units(w):
        rows = w.shape[0]
        return lax.dynamic_index_in_dim(
            w.reshape(rows, shards, 2, -1), rep, axis=2, keepdims=False
        ).reshape(rows, -1)

    def collect(layer):
        _, q, k, v, o, _, g, u, d = layer
        wide = (q.shape[1] + k.shape[1] + v.shape[1]) // 2
        packed = jnp.concatenate([columns(q), columns(k), columns(v), columns(o)], axis=1)
        down_half = lax.dynamic_slice_in_dim(d, rep * (d.shape[0] // 2), d.shape[0] // 2, 0)
        packed, g, u, d = (
            gather(w) for w in (packed, hidden_units(g), hidden_units(u), down_half)
        )
        packed, g, u, d = ((w, swap(w)) for w in (packed, g, u, d))
        return (
            tuple(w[:, :wide] for w in packed),
            tuple(w[:, wide:] for w in packed),
            g,
            u,
            d,
        )

    hidden = inputs[0].astype(F32)
    weights = [collect(layer) for layer in layers]
    saved = [None, None]
    for n in (0, 1):
        gains = (all_gains[2 * n], all_gains[2 * n + 1])
        hidden, saved[n] = layer_forward(hidden, gains, weights[n], tables, first)
    flow = cotangent[0].astype(F32)
    gain_grads, grads = [None, None], [None, None]
    for n in (1, 0):
        gains = (all_gains[2 * n], all_gains[2 * n + 1])
        flow, gain_grads[n], grads[n] = layer_backward(
            flow, gains, weights[n], saved[n], tables, first
        )
    gain_rows = jnp.stack([g for pair in gain_grads for g in pair])
    gain_rows = lax.psum(gain_rows, ("rep",) + GROUP)
    own_rows = width // shards
    gain_rows = lax.dynamic_slice_in_dim(gain_rows, position_of * own_rows, own_rows, 1)

    results = []
    for n in (0, 1):
        _, q, k, v, o, _, g, u, d = layers[n]
        attn, gate, up, down = grads[n]
        packs = arrange(first, attn, swap(attn))
        gates = arrange(first, gate, swap(gate))
        ups = arrange(first, up, swap(up))
        downs = arrange(first, down, swap(down))
        edges = [0]
        for w in (q, k, v, o):
            edges.append(edges[-1] + w.shape[1] // 2)
        q, k, v, o = (
            jnp.concatenate([p[:, a:b] for p in packs], axis=1).astype(F32)
            for a, b in zip(edges[:-1], edges[1:])
        )
        g, u = (
            jnp.stack([p.reshape(own_rows, shards, -1) for p in pair], axis=2)
            .reshape(own_rows, -1)
            .astype(F32)
            for pair in (gates, ups)
        )
        d = jnp.concatenate(downs, axis=0).astype(F32)
        results += [gain_rows[2 * n], q, k, v, o, gain_rows[2 * n + 1], g, u, d]
    return (hidden[None], flow[None], *results)


def solution(mesh):
    tokens = P(("rep", "shard"), "ctx", None)
    vector, matrix = P(GROUP), P(GROUP, None)
    layer = (vector, matrix, matrix, matrix, matrix, vector, matrix, matrix, matrix)
    return jax.shard_map(
        body,
        mesh=mesh,
        in_specs=(tokens, P(("rep", "shard"), "ctx"), tokens) + layer + layer,
        out_specs=(tokens, tokens) + layer + layer,
        check_vma=False,
    )
```
